32 devices in a mesh: gx: 16 (over z, x, core), gy: 2 (over y).
Axes of the slice: x: 2, y: 2, z: 4, core: 2. Of those that a mesh axis runs over, the one named last changes fastest.
Arguments:
- volume_field: float32 [3, 256, 32, 128], P(None, 'gx', 'gy'), may hold values from -6 to 6
- diag_blocks: float32 [3, 3, 256, 32, 128], P(None, None, 'gx', 'gy'), may hold values from -4 to 4
- face_weights: float32 [6, 2, 256, 32, 128], P(None, None, 'gx', 'gy'), may hold values from 0.3 to 3
- boundary_field: float32 [16, 2, 1536], P('gx', 'gy'), may hold values from -6 to 6
- self_term: float32 [16, 2, 1536], P('gx', 'gy'), may hold values from 0.5 to 2
- coupling: float32 [16, 2, 1536], P('gx', 'gy'), may hold values from 0.3 to 3
- owner_map: int32 [16, 2, 1536], P('gx', 'gy'), may hold values from 0 to 1535, as said below
- left_basis: bfloat16 [32, 16, 2, 1536], P('gy', 'gx'), may hold values from -1 to 1
- right_basis: bfloat16 [256, 16, 2, 1536], P('gx', None, 'gy'), may hold values from -0.0390625 to 0.0390625
Outputs:
- volume_out: float32 [3, 256, 32, 128], P(None, 'gx', 'gy')
- boundary_out: float32 [16, 2, 1536], P('gx', 'gy')
The draws below stay inside these ranges and needn't reach their ends.
Inputs may be any that keep to these rules, and one draw needn't show every extreme that they name: `owner_map`: within each subdomain (p, q) the 1536 entries name every surface edge of that subdomain exactly once.
All inputs are finite; a program needn't handle non-finite values.
Results may differ from the reference program's by a relative error of at most 0.0017.
Values may be sent and summed in bfloat16 or wider, within the bound.
No kernel may reach another device: no remote copies, remote signals or barrier semaphores. Data moves between devices by JAX's collectives and lax.ppermute only.
A program may use at most 64 MiB of HBM per device.

```python
import math
import jax
import jax.numpy as jnp
from jax import lax

CX = 16
CY = 16
NZ = 128
R = 16
NX = 256
NY = 32
NB_DEV = 1536
N_GX = 16
N_GY = 2


def draw_owner_map(key, part):
    keys = jax.random.split(jax.random.fold_in(key, 17), N_GX * N_GY)
    perms = jax.vmap(lambda single: jax.random.permutation(single, NB_DEV))(keys)
    return perms.reshape(N_GX, N_GY, NB_DEV).astype(jnp.int32)


def block_scale(key, dims, cuts, smallest, top_value):
    def one(position, shards_of):
        draws = jax.random.uniform(jax.random.fold_in(jax.random.fold_in(key, 6), position), (shards_of,), jnp.float32, smallest / len(cuts), top_value / len(cuts))
        return jnp.repeat(jnp.exp(draws), dims[position] // shards_of).reshape((-1,) + (1,) * (len(dims) - position - 1))

    loudness = one(*cuts[0])
    for cut in cuts[1:]:
        loudness = loudness * one(*cut)
    return loudness


def normal_values(rng, dims, scale, limit, shards=(), dtype=jnp.bfloat16):
    loudness = block_scale(rng, dims, shards, -0.22, 0.18) if shards else 1.0
    drawn = jax.random.normal(rng, dims, jnp.float32) * scale * loudness
    return jnp.minimum(jnp.maximum(drawn, -limit), limit).astype(dtype)


def setup_inputs(seed: int = 0) -> dict:
    key_of = jax.random.split(jax.random.key(seed), 10)
    volume_field = normal_values(key_of[0], (3, NX, NY, NZ), 1.0, 6.0, ((1, 16), (2, 2)), jnp.float32)
    diag_blocks = normal_values(key_of[1], (3, 3, NX, NY, NZ), 1.0, 4.0, ((2, 16), (3, 2)), jnp.float32)
    face_weights = jnp.clip(jnp.exp(math.log(3.0) - 2.3025851 * jax.random.uniform(key_of[2], (6, 2, NX, NY, NZ), jnp.float32) ** block_scale(key_of[2], (6, 2, NX, NY, NZ), ((2, 16), (3, 2)), -0.2, 0.2)), 0.3, 3.0)
    boundary_field = normal_values(key_of[3], (N_GX, N_GY, NB_DEV), 1.0, 6.0, ((0, 16), (1, 2)), jnp.float32)
    self_term = jnp.clip(0.5 + 1.5 * jax.random.uniform(key_of[4], (N_GX, N_GY, NB_DEV), jnp.float32) ** block_scale(key_of[4], (N_GX, N_GY, NB_DEV), ((0, 16), (1, 2)), -0.2, 0.2), 0.5, 2.0)
    coupling = jnp.clip(jnp.exp(math.log(3.0) - 2.3025851 * jax.random.uniform(key_of[5], (N_GX, N_GY, NB_DEV), jnp.float32) ** block_scale(key_of[5], (N_GX, N_GY, NB_DEV), ((0, 16), (1, 2)), -0.2, 0.2)), 0.3, 3.0)
    owner_map = draw_owner_map(jax.random.fold_in(key_of[9], 71), 0)
    left_basis = normal_values(key_of[7], (N_GY * R, N_GX, N_GY, NB_DEV), (N_GY * R) ** -0.5, 1.0, ((0, 2), (1, 16)))
    right_basis = normal_values(key_of[8], (N_GX * R, N_GX, N_GY, NB_DEV), (N_GX * NB_DEV) ** -0.5, 0.0390625, ((0, 16), (2, 2)))
    return dict(volume_field=volume_field, diag_blocks=diag_blocks, face_weights=face_weights, boundary_field=boundary_field, self_term=self_term, coupling=coupling, owner_map=owner_map, left_basis=left_basis, right_basis=right_basis)


def apply_blocks(field_in, diag_blocks, face_weights, neighbours):
    comp_rows = []
    for comp in range(3):
        accum_row = diag_blocks[comp, 0] * field_in[0] + diag_blocks[comp, 1] * field_in[1] + diag_blocks[comp, 2] * field_in[2]
        comp_rows.append(accum_row)
    for offset in range(6):
        direction = offset // 2
        tangent = [comp for comp in range(3) if comp != direction]
        for slot in range(2):
            comp_rows[tangent[slot]] = comp_rows[tangent[slot]] - face_weights[offset, slot] * neighbours[offset][slot]
    return jnp.stack(comp_rows)


def reference(volume_field, diag_blocks, face_weights, boundary_field, self_term, coupling, owner_map, left_basis, right_basis):
    padded = jnp.pad(volume_field, ((0, 0), (1, 1), (1, 1), (1, 1)))
    neighbours = [padded[1:3, 2:, 1:-1, 1:-1], padded[1:3, :-2, 1:-1, 1:-1],
                  padded[0::2, 1:-1, 2:, 1:-1], padded[0::2, 1:-1, :-2, 1:-1],
                  padded[0:2, 1:-1, 1:-1, 2:], padded[0:2, 1:-1, 1:-1, :-2]]
    stiffness = apply_blocks(volume_field, diag_blocks, face_weights, neighbours)
    surface_rows = jnp.stack([volume_field[..., 0], volume_field[..., -1]])
    surface = surface_rows.reshape(2, 3, N_GX, CX, N_GY, CY).transpose(2, 4, 0, 1, 3, 5).reshape(N_GX, N_GY, NB_DEV)
    edge_trace = jnp.take_along_axis(surface, owner_map, axis=2)

    def place_one(index_row, value_row):
        return jnp.zeros_like(value_row).at[index_row].set(value_row)

    placed = jax.vmap(jax.vmap(place_one))(owner_map, coupling * boundary_field)
    placed = placed.reshape(N_GX, N_GY, 2, 3, CX, CY).transpose(2, 3, 0, 4, 1, 5).reshape(2, 3, NX, NY)
    volume_out = stiffness.at[:, :, :, 0].add(placed[0]).at[:, :, :, -1].add(placed[1])

    boundary_half = lax.optimization_barrier(boundary_field.astype(jnp.bfloat16))
    right_split = right_basis.reshape(N_GX, R, N_GX, N_GY, NB_DEV)

    def project(basis_block):
        return jnp.einsum('rxbk,xbk->br', basis_block.astype(jnp.float32), boundary_half.astype(jnp.float32))

    coef = lax.map(project, right_split)
    coef_half = lax.optimization_barrier(coef.astype(jnp.bfloat16))
    left_split = left_basis.reshape(N_GY, R, N_GX, N_GY, NB_DEV).transpose(2, 0, 1, 3, 4)

    def expand(pair):
        basis_block, coef_block = pair
        return jnp.einsum('yrbk,yr->bk', basis_block.astype(jnp.float32), coef_block.astype(jnp.float32))

    integral = lax.map(expand, (left_split, coef_half))
    boundary_out = self_term * boundary_field + integral + coupling * edge_trace
    return volume_out, boundary_out
```

```python
import functools

import jax
import jax.numpy as jnp
from jax import lax
from jax.experimental import pallas as pl
from jax.experimental.pallas import tpu as pltpu
from jax.sharding import PartitionSpec as P

LANES = 128
NT = (((1,), (1,)), ((), ()))


def split3(value):
    top = value.astype(jnp.bfloat16)
    rest = value - top.astype(jnp.float32)
    mid = rest.astype(jnp.bfloat16)
    low = (rest - mid.astype(jnp.float32)).astype(jnp.bfloat16)
    return top, mid, low


def payload_kernel(x_index, y_index, field, boundary, core_out, outer_out, y_out):
    rows = boundary.shape[1] // LANES
    head = core_out.shape[0] - outer_out.shape[0]
    cells_x, cells_y = field.shape[1], field.shape[2]
    even_x = x_index[0] % 2 == 0
    even_y = y_index[0] % 2 == 0
    inner = jnp.where(even_x, cells_x - 1, 0)
    outer = cells_x - 1 - inner
    core_out[0:head, :] = jnp.zeros((head, LANES), jnp.float32)
    for q in range(rows):
        core_out[q : q + 1, :] = boundary[:, q * LANES : (q + 1) * LANES]
    for slot, comp in enumerate((1, 2)):
        at = slot * cells_y
        core_out[head + at : head + at + cells_y, :] = field[comp, inner]
        outer_out[at : at + cells_y, :] = field[comp, outer]
    for slot, comp in enumerate((0, 2)):
        for x in range(cells_x):
            high = field[comp, x, cells_y - 1 : cells_y, :]
            low = field[comp, x, 0:1, :]
            at = slot * cells_x + x
            y_out[0, at : at + 1, :] = jnp.where(even_y, high, low)
            if y_out.shape[0] == 2:
                y_out[1, at : at + 1, :] = jnp.where(even_y, low, high)


def volume_kernel(
    x_index,
    y_index,
    field,
    diag,
    face,
    x_inner,
    x_outer,
    y_halo,
    boundary,
    self_term,
    coupling,
    owner,
    volume_out,
    base_out,
):
    _, cells_x, cells_y, cells_z = field.shape
    count = boundary.shape[1]
    blocks = count // LANES
    half = blocks // 2
    per_block = LANES // cells_y
    padded = -(-blocks // 16) * 16
    head = x_inner.shape[0] - x_outer.shape[0]
    even_x = x_index[0] % 2 == 0
    even_y = y_index[0] % 2 == 0

    slot_of = owner[...]
    lane_of = slot_of % LANES
    block_of = slot_of // LANES
    onehot = (
        (lane_of == lax.broadcasted_iota(jnp.int32, (LANES, count), 0))
        .astype(jnp.float32)
        .astype(jnp.bfloat16)
    )
    in_block = block_of == lax.broadcasted_iota(jnp.int32, (padded, count), 0)

    spread = jnp.where(in_block, coupling[...] * boundary[...], 0.0)
    placed = jnp.zeros((LANES, padded), jnp.float32)
    for term in split3(spread):
        placed += lax.dot_general(onehot, term, NT, preferred_element_type=jnp.float32)

    ends = lax.broadcasted_iota(jnp.int32, (16, cells_z), 0)
    lane = lax.broadcasted_iota(jnp.int32, (16, cells_z), 1)
    pick = (
        (((ends == 0) & (lane == 0)) | ((ends == 1) & (lane == cells_z - 1)))
        .astype(jnp.float32)
        .astype(jnp.bfloat16)
    )
    flat = field[...].reshape(3 * cells_x * cells_y, cells_z)
    surface = jnp.zeros((16, 3 * cells_x * cells_y), jnp.float32)
    for term in split3(flat):
        surface += lax.dot_general(pick, term, NT, preferred_element_type=jnp.float32)
    table = jnp.concatenate(
        [
            surface[e : e + 1, b * LANES : (b + 1) * LANES]
            for e in range(2)
            for b in range(half)
        ]
        + [jnp.zeros((padded - blocks, LANES), jnp.float32)],
        axis=0,
    )
    read = jnp.zeros((padded, count), jnp.float32)
    for term in split3(table):
        read += jnp.dot(term, onehot, preferred_element_type=jnp.float32)
    trace = jnp.sum(jnp.where(in_block, read, 0.0), axis=0, keepdims=True)
    base_out[...] = self_term[...] * boundary[...] + coupling[...] * trace

    z_at = lax.broadcasted_iota(jnp.int32, (cells_y, cells_z), 1)
    y_at = lax.broadcasted_iota(jnp.int32, (cells_y, cells_z), 0)
    first_z, last_z = z_at == 0, z_at == cells_z - 1
    first_y, last_y = y_at == 0, y_at == cells_y - 1
    for x in range(cells_x):
        own = [field[c, x] for c in range(3)]
        x_plus, x_minus = {}, {}
        for slot, comp in enumerate((1, 2)):
            near = x_inner[head + slot * cells_y : head + (slot + 1) * cells_y, :]
            far = x_outer[slot * cells_y : (slot + 1) * cells_y, :]
            if x + 1 < cells_x:
                x_plus[comp] = field[comp, x + 1]
            else:
                x_plus[comp] = jnp.where(even_x, near, far)
            if x > 0:
                x_minus[comp] = field[comp, x - 1]
            else:
                x_minus[comp] = jnp.where(even_x, far, near)
        y_plus, y_minus = {}, {}
        for slot, comp in enumerate((0, 2)):
            at = slot * cells_x + x
            near = y_halo[0, at : at + 1, :]
            if y_halo.shape[0] == 2:
                far = y_halo[1, at : at + 1, :]
            else:
                far = jnp.zeros_like(near)
            above = jnp.where(even_y, near, far)
            below = jnp.where(even_y, far, near)
            y_plus[comp] = jnp.where(last_y, above, pltpu.roll(own[comp], cells_y - 1, 0))
            y_minus[comp] = jnp.where(first_y, below, pltpu.roll(own[comp], 1, 0))
        z_plus, z_minus = {}, {}
        for comp in (0, 1):
            z_plus[comp] = jnp.where(last_z, 0.0, pltpu.roll(own[comp], cells_z - 1, 1))
            z_minus[comp] = jnp.where(first_z, 0.0, pltpu.roll(own[comp], 1, 1))
        total = []
        for comp in range(3):
            total.append(
                diag[comp, 0, x] * own[0] + diag[comp, 1, x] * own[1] + diag[comp, 2, x] * own[2]
            )
        steps = (x_plus, x_minus, y_plus, y_minus, z_plus, z_minus)
        for offset, step in enumerate(steps):
            direction = offset // 2
            for slot, comp in enumerate(c for c in range(3) if c != direction):
                total[comp] = total[comp] - face[offset, slot, x] * step[comp]
        for comp in range(3):
            row = (comp * cells_x + x) * cells_y
            block, at = row // LANES, row % LANES
            bottom = placed[at : at + cells_y, block : block + 1]
            top = placed[at : at + cells_y, half + block : half + block + 1]
            total[comp] = total[comp] + jnp.where(
                first_z, bottom, jnp.where(last_z, top, 0.0)
            )
            volume_out[comp, x] = total[comp]


def integral_kernel(x_index, y_index, mine, theirs, right, left, base, own_out, send_out, stack, partial_value):
    columns = left.shape[1]
    rank, groups = right.shape[0], right.shape[1]
    count = right.shape[2]
    held = mine.shape[0]
    pitch = mine.shape[1]
    stack[0 : held * pitch, :] = mine[...].astype(jnp.float32).reshape(held * pitch, LANES)
    stack[held * pitch :, :] = theirs[...].astype(jnp.float32).reshape(held * pitch, LANES)
    pieces = [stack[pl.ds(q, groups, stride=pitch), :] for q in range(count // LANES)]
    gathered = jnp.concatenate(pieces, axis=1).astype(jnp.bfloat16)
    table = right[...].reshape(rank * groups, count)
    product = lax.dot_general(table, gathered, NT, preferred_element_type=jnp.float32)
    product = product.reshape(rank, groups, groups)
    source = lax.broadcasted_iota(jnp.int32, (rank, groups, groups), 2) ^ x_index[0]
    group = lax.broadcasted_iota(jnp.int32, (rank, groups, groups), 1)
    product = jnp.where(source == group, product, 0.0)
    coef = jnp.sum(jnp.sum(product, axis=1, keepdims=True), axis=2, keepdims=True)
    coef = coef.astype(jnp.bfloat16).astype(jnp.float32)
    total = jnp.zeros((columns, count), jnp.float32)
    for r in range(rank):
        total = total + coef[r] * left[r].astype(jnp.float32)
    partial_value[...] = total
    me = y_index[0]
    own_out[...] = base[...] + partial_value[pl.ds(me, 1), :]
    for step in range(1, columns):
        to = lax.rem(me + step, columns)
        send_out[step - 1] = partial_value[pl.ds(to, 1), :]


def on_device(
    n_x,
    n_y,
    volume_field,
    diag_blocks,
    face_weights,
    boundary_field,
    self_term,
    coupling,
    owner_map,
    left_basis,
    right_basis,
):
    f32 = jnp.float32
    _, cells_x, cells_y, cells_z = volume_field.shape
    count = boundary_field.shape[2]
    rank = left_basis.shape[0]
    rows = count // LANES
    head = -(-rows // 16) * 16
    x_index = lax.axis_index("gx").reshape(1)
    y_index = lax.axis_index("gy").reshape(1)
    boundary = boundary_field.reshape(1, count)
    vmem = pl.BlockSpec(memory_space=pltpu.VMEM)
    smem = pl.BlockSpec(memory_space=pltpu.SMEM)
    y_sides = 1 if n_y == 2 else 2

    def call(body, outs, n_in, scratch=()):
        return pl.pallas_call(
            body,
            out_shape=outs,
            in_specs=[smem, smem] + [vmem] * n_in,
            out_specs=[vmem] * len(outs),
            scratch_shapes=scratch,
            name=body.__name__,
        )

    def inner_pairs(size):
        return [(i, i ^ 1) for i in range(size)]

    def outer_pairs(size):
        up = [(i, i + 1) for i in range(1, size - 1, 2)]
        return up + [(j, i) for i, j in up]

    core_pay, outer_pay, y_pay = call(
        payload_kernel,
        [
            jax.ShapeDtypeStruct((head + 2 * cells_y, LANES), f32),
            jax.ShapeDtypeStruct((2 * cells_y, LANES), f32),
            jax.ShapeDtypeStruct((y_sides, 2 * cells_x, LANES), f32),
        ],
        2,
    )(x_index, y_index, volume_field, boundary)

    core_got = lax.ppermute(core_pay, "gx", inner_pairs(n_x))
    x_outer = lax.ppermute(outer_pay, "gx", outer_pairs(n_x))
    y_halo = lax.ppermute(y_pay[0], "gy", inner_pairs(n_y))[None]
    if y_sides == 2:
        y_far = lax.ppermute(y_pay[1], "gy", outer_pairs(n_y))[None]
        y_halo = jnp.concatenate([y_halo, y_far], axis=0)

    mine = core_pay[:head].astype(jnp.bfloat16)[None]
    theirs = core_got[:head].astype(jnp.bfloat16)[None]
    step = 2
    while step < n_x:
        mine = jnp.concatenate([mine, theirs], axis=0)
        theirs = lax.ppermute(mine, "gx", [(i, i ^ step) for i in range(n_x)])
        step *= 2

    volume_out, base = call(
        volume_kernel,
        [
            jax.ShapeDtypeStruct(volume_field.shape, f32),
            jax.ShapeDtypeStruct((1, count), f32),
        ],
        10,
    )(
        x_index,
        y_index,
        volume_field,
        diag_blocks,
        face_weights,
        core_got,
        x_outer,
        y_halo,
        boundary,
        self_term.reshape(1, count),
        coupling.reshape(1, count),
        owner_map.reshape(1, count),
    )

    own, send = call(
        integral_kernel,
        [
            jax.ShapeDtypeStruct((1, count), f32),
            jax.ShapeDtypeStruct((n_y - 1, 1, count), f32),
        ],
        5,
        [
            pltpu.VMEM((n_x * head, LANES), f32),
            pltpu.VMEM((n_y, count), f32),
        ],
    )(
        x_index,
        y_index,
        mine,
        theirs,
        right_basis.reshape(rank, n_x, count),
        left_basis.reshape(rank, n_y, count),
        base,
    )
    total = own
    for shift in range(1, n_y):
        pairs = [(i, (i + shift) % n_y) for i in range(n_y)]
        total = total + lax.ppermute(send[shift - 1], "gy", pairs)
    return volume_out, total.reshape(boundary_field.shape)


def solution(mesh):
    body = functools.partial(on_device, mesh.shape["gx"], mesh.shape["gy"])
    return jax.shard_map(
        body,
        mesh=mesh,
        in_specs=(
            P(None, "gx", "gy", None),
            P(None, None, "gx", "gy", None),
            P(None, None, "gx", "gy", None),
            P("gx", "gy", None),
            P("gx", "gy", None),
            P("gx", "gy", None),
            P("gx", "gy", None),
            P("gy", "gx", None, None),
            P("gx", None, "gy", None),
        ),
        out_specs=(P(None, "gx", "gy", None), P("gx", "gy", None)),
        check_vma=False,
    )
```

```python
import functools

import jax
import jax.numpy as jnp
from jax import lax
from jax.experimental import pallas as pl
from jax.experimental.pallas import tpu as pltpu
from jax.sharding import PartitionSpec as P

LANES = 128
NT = (((1,), (1,)), ((), ()))


def split3(value):
    top = value.astype(jnp.bfloat16)
    rest = value - top.astype(jnp.float32)
    mid = rest.astype(jnp.bfloat16)
    low = (rest - mid.astype(jnp.float32)).astype(jnp.bfloat16)
    return top, mid, low


def halo_kernel(
    x_index, y_index, field, boundary, inner_out, outer_out, y_out, boundary_out, sems
):
    cells_x, cells_y = field.shape[1], field.shape[2]
    inner = jnp.where(x_index[0] % 2 == 0, cells_x - 1, 0)
    beside = jnp.where(y_index[0] % 2 == 0, cells_y - 1, 0)
    copies = []

    def copy(source, target):
        copies.append(pltpu.make_async_copy(source, target, sems.at[len(copies)]))
        copies[-1].start()

    for slot, comp in enumerate((1, 2)):
        rows = pl.ds(slot * cells_y, cells_y)
        copy(field.at[comp, inner], inner_out.at[rows])
        copy(field.at[comp, cells_x - 1 - inner], outer_out.at[rows])
    for side in range(y_out.shape[0]):
        row = beside if side == 0 else cells_y - 1 - beside
        for slot, comp in enumerate((0, 2)):
            rows = pl.ds(slot * cells_x, cells_x)
            copy(field.at[comp, :, row], y_out.at[side, rows])
    copy(boundary, boundary_out)
    for one in copies:
        one.wait()


def pack_kernel(mine, theirs, out):
    rows = mine.shape[1] // LANES
    for i, source in enumerate((mine, theirs)):
        lines = [source[:, q * LANES : (q + 1) * LANES] for q in range(rows)]
        lines.append(jnp.zeros((out.shape[1] - rows, LANES), jnp.float32))
        out[i] = jnp.concatenate(lines, axis=0).astype(jnp.bfloat16)


def volume_kernel(
    x_index,
    y_index,
    field_in,
    diag_in,
    face_in,
    boundary_in,
    self_in,
    coupling_in,
    owner_in,
    x_inner,
    x_outer,
    y_halo,
    volume_out,
    base_out,
    field,
    diag,
    face,
    boundary,
    self_term,
    coupling,
    owner,
    sems,
):
    pairs = (
        (owner_in, owner),
        (coupling_in, coupling),
        (boundary_in, boundary),
        (self_in, self_term),
        (field_in, field),
        (diag_in, diag),
        (face_in, face),
    )
    loads = [pltpu.make_async_copy(a, b, sems.at[i]) for i, (a, b) in enumerate(pairs)]
    for load in loads:
        load.start()
    _, cells_x, cells_y, cells_z = field.shape
    count = boundary.shape[1]
    blocks = count // LANES
    half = blocks // 2
    padded = -(-blocks // 16) * 16
    even_x = x_index[0] % 2 == 0
    even_y = y_index[0] % 2 == 0

    for load in loads[:4]:
        load.wait()

    slot_of = owner[...]
    lane_of = slot_of % LANES
    block_of = slot_of // LANES
    onehot = (
        (lane_of == lax.broadcasted_iota(jnp.int32, (LANES, count), 0))
        .astype(jnp.float32)
        .astype(jnp.bfloat16)
    )
    in_block = block_of == lax.broadcasted_iota(jnp.int32, (padded, count), 0)

    spread = jnp.where(in_block, coupling[...] * boundary[...], 0.0)
    placed = jnp.zeros((LANES, padded), jnp.float32)
    for term in split3(spread):
        placed += lax.dot_general(onehot, term, NT, preferred_element_type=jnp.float32)

    ends = lax.broadcasted_iota(jnp.int32, (16, cells_z), 0)
    lane = lax.broadcasted_iota(jnp.int32, (16, cells_z), 1)
    pick = (
        (((ends == 0) & (lane == 0)) | ((ends == 1) & (lane == cells_z - 1)))
        .astype(jnp.float32)
        .astype(jnp.bfloat16)
    )
    loads[4].wait()
    flat = field[...].reshape(3 * cells_x * cells_y, cells_z)
    surface = jnp.zeros((16, 3 * cells_x * cells_y), jnp.float32)
    for term in split3(flat):
        surface += lax.dot_general(pick, term, NT, preferred_element_type=jnp.float32)
    table = jnp.concatenate(
        [
            surface[e : e + 1, b * LANES : (b + 1) * LANES]
            for e in range(2)
            for b in range(half)
        ]
        + [jnp.zeros((padded - blocks, LANES), jnp.float32)],
        axis=0,
    )
    read = jnp.zeros((padded, count), jnp.float32)
    for term in split3(table):
        read += jnp.dot(term, onehot, preferred_element_type=jnp.float32)
    trace = jnp.sum(jnp.where(in_block, read, 0.0), axis=0, keepdims=True)
    base_out[...] = self_term[...] * boundary[...] + coupling[...] * trace

    for load in loads[5:]:
        load.wait()
    z_at = lax.broadcasted_iota(jnp.int32, (cells_y, cells_z), 1)
    y_at = lax.broadcasted_iota(jnp.int32, (cells_y, cells_z), 0)
    first_z, last_z = z_at == 0, z_at == cells_z - 1
    first_y, last_y = y_at == 0, y_at == cells_y - 1
    for x in range(cells_x):
        own = [field[c, x] for c in range(3)]
        x_plus, x_minus = {}, {}
        for slot, comp in enumerate((1, 2)):
            near = x_inner[slot * cells_y : (slot + 1) * cells_y, :]
            far = x_outer[slot * cells_y : (slot + 1) * cells_y, :]
            if x + 1 < cells_x:
                x_plus[comp] = field[comp, x + 1]
            else:
                x_plus[comp] = jnp.where(even_x, near, far)
            if x > 0:
                x_minus[comp] = field[comp, x - 1]
            else:
                x_minus[comp] = jnp.where(even_x, far, near)
        y_plus, y_minus = {}, {}
        for slot, comp in enumerate((0, 2)):
            at = slot * cells_x + x
            near = y_halo[0, at : at + 1, :]
            if y_halo.shape[0] == 2:
                far = y_halo[1, at : at + 1, :]
            else:
                far = jnp.zeros_like(near)
            above = jnp.where(even_y, near, far)
            below = jnp.where(even_y, far, near)
            y_plus[comp] = jnp.where(last_y, above, pltpu.roll(own[comp], cells_y - 1, 0))
            y_minus[comp] = jnp.where(first_y, below, pltpu.roll(own[comp], 1, 0))
        z_plus, z_minus = {}, {}
        for comp in (0, 1):
            z_plus[comp] = jnp.where(last_z, 0.0, pltpu.roll(own[comp], cells_z - 1, 1))
            z_minus[comp] = jnp.where(first_z, 0.0, pltpu.roll(own[comp], 1, 1))
        total = []
        for comp in range(3):
            total.append(
                diag[comp, 0, x] * own[0] + diag[comp, 1, x] * own[1] + diag[comp, 2, x] * own[2]
            )
        steps = (x_plus, x_minus, y_plus, y_minus, z_plus, z_minus)
        for offset, step in enumerate(steps):
            direction = offset // 2
            for slot, comp in enumerate(c for c in range(3) if c != direction):
                total[comp] = total[comp] - face[offset, slot, x] * step[comp]
        for comp in range(3):
            row = (comp * cells_x + x) * cells_y
            block, at = row // LANES, row % LANES
            bottom = placed[at : at + cells_y, block : block + 1]
            top = placed[at : at + cells_y, half + block : half + block + 1]
            total[comp] = total[comp] + jnp.where(
                first_z, bottom, jnp.where(last_z, top, 0.0)
            )
            volume_out[comp, x] = total[comp]


def integral_kernel(x_index, y_index, mine, theirs, right, left, base, own_out, send_out, stack, partial_value):
    columns = left.shape[1]
    rank, groups = right.shape[0], right.shape[1]
    count = right.shape[2]
    held = mine.shape[0]
    pitch = mine.shape[1]
    stack[0 : held * pitch, :] = mine[...].astype(jnp.float32).reshape(held * pitch, LANES)
    stack[held * pitch :, :] = theirs[...].astype(jnp.float32).reshape(held * pitch, LANES)
    pieces = [stack[pl.ds(q, groups, stride=pitch), :] for q in range(count // LANES)]
    gathered = jnp.concatenate(pieces, axis=1).astype(jnp.bfloat16)
    table = right[...].reshape(rank * groups, count)
    product = lax.dot_general(table, gathered, NT, preferred_element_type=jnp.float32)
    product = product.reshape(rank, groups, groups)
    source = lax.broadcasted_iota(jnp.int32, (rank, groups, groups), 2) ^ x_index[0]
    group = lax.broadcasted_iota(jnp.int32, (rank, groups, groups), 1)
    product = jnp.where(source == group, product, 0.0)
    coef = jnp.sum(jnp.sum(product, axis=1, keepdims=True), axis=2, keepdims=True)
    coef = coef.astype(jnp.bfloat16).astype(jnp.float32)
    total = jnp.zeros((columns, count), jnp.float32)
    for r in range(rank):
        total = total + coef[r] * left[r].astype(jnp.float32)
    partial_value[...] = total
    me = y_index[0]
    own_out[...] = base[...] + partial_value[pl.ds(me, 1), :]
    for step in range(1, columns):
        to = lax.rem(me + step, columns)
        send_out[step - 1] = partial_value[pl.ds(to, 1), :]


def on_device(
    n_x,
    n_y,
    volume_field,
    diag_blocks,
    face_weights,
    boundary_field,
    self_term,
    coupling,
    owner_map,
    left_basis,
    right_basis,
):
    f32 = jnp.float32
    _, cells_x, cells_y, _ = volume_field.shape
    count = boundary_field.shape[2]
    rank = left_basis.shape[0]
    rows = count // LANES
    head = -(-rows // 16) * 16
    x_index = lax.axis_index("gx").reshape(1)
    y_index = lax.axis_index("gy").reshape(1)
    boundary = boundary_field.reshape(1, count)
    vmem = pl.BlockSpec(memory_space=pltpu.VMEM)
    smem = pl.BlockSpec(memory_space=pltpu.SMEM)
    hbm = pl.BlockSpec(memory_space=pltpu.HBM)
    y_sides = 1 if n_y == 2 else 2

    def call(body, outs, args, scratch=(), far=0, indices=True):
        lead = (x_index, y_index) if indices else ()
        args = [
            pltpu.with_memory_space_constraint(arg, pltpu.HBM if i < far else pltpu.VMEM)
            for i, arg in enumerate(args)
        ]
        return pl.pallas_call(
            body,
            out_shape=outs,
            in_specs=[smem] * len(lead) + [hbm] * far + [vmem] * (len(args) - far),
            out_specs=[vmem] * len(outs),
            scratch_shapes=scratch,
            compiler_params=pltpu.CompilerParams(vmem_limit_bytes=16 * 2**20),
        )(*lead, *args)

    def inner_pairs(size):
        return [(i, i ^ 1) for i in range(size)]

    def outer_pairs(size):
        up = [(i, i + 1) for i in range(1, size - 1, 2)]
        return up + [(j, i) for i, j in up]

    core_got = lax.ppermute(boundary, "gx", inner_pairs(n_x))
    inner_pay, outer_pay, y_pay, near_boundary = call(
        halo_kernel,
        [
            pltpu.VMEM((2 * cells_y, LANES), f32),
            pltpu.VMEM((2 * cells_y, LANES), f32),
            pltpu.VMEM((y_sides, 2 * cells_x, LANES), f32),
            pltpu.VMEM((1, count), f32),
        ],
        [volume_field, boundary],
        [pltpu.SemaphoreType.DMA((5 + 2 * y_sides,))],
        far=2,
    )
    x_inner = lax.ppermute(inner_pay, "gx", inner_pairs(n_x))
    x_outer = lax.ppermute(outer_pay, "gx", outer_pairs(n_x))
    y_halo = lax.ppermute(y_pay[0], "gy", inner_pairs(n_y))[None]
    if y_sides == 2:
        y_far = lax.ppermute(y_pay[1], "gy", outer_pairs(n_y))[None]
        y_halo = jnp.concatenate([y_halo, y_far], axis=0)

    (mine,) = call(
        pack_kernel,
        [pltpu.VMEM((2, head, LANES), jnp.bfloat16)],
        [near_boundary, core_got],
        indices=False,
    )
    theirs = lax.ppermute(mine, "gx", [(i, i ^ 2) for i in range(n_x)])
    step = 4
    while step < n_x:
        mine = jnp.concatenate([mine, theirs], axis=0)
        theirs = lax.ppermute(mine, "gx", [(i, i ^ step) for i in range(n_x)])
        step *= 2

    row = (1, count)
    volume_out, base = call(
        volume_kernel,
        [pltpu.VMEM(volume_field.shape, f32), pltpu.VMEM(row, f32)],
        [
            volume_field,
            diag_blocks,
            face_weights,
            boundary,
            self_term.reshape(row),
            coupling.reshape(row),
            owner_map.reshape(row),
            x_inner,
            x_outer,
            y_halo,
        ],
        [
            pltpu.VMEM(volume_field.shape, f32),
            pltpu.VMEM(diag_blocks.shape, f32),
            pltpu.VMEM(face_weights.shape, f32),
            pltpu.VMEM(row, f32),
            pltpu.VMEM(row, f32),
            pltpu.VMEM(row, f32),
            pltpu.VMEM(row, jnp.int32),
            pltpu.SemaphoreType.DMA((7,)),
        ],
        far=7,
    )

    own, shares = call(
        integral_kernel,
        [
            pltpu.VMEM((1, count), f32),
            pltpu.VMEM((n_y - 1, 1, count), f32),
        ],
        [
            mine,
            theirs,
            right_basis.reshape(rank, n_x, count),
            left_basis.reshape(rank, n_y, count),
            base,
        ],
        [
            pltpu.VMEM((n_x * head, LANES), f32),
            pltpu.VMEM((n_y, count), f32),
        ],
    )
    total = own
    for shift in range(1, n_y):
        pairs = [(i, (i + shift) % n_y) for i in range(n_y)]
        total = total + lax.ppermute(shares[shift - 1], "gy", pairs)
    return volume_out, total.reshape(boundary_field.shape)


def solution(mesh):
    body = functools.partial(on_device, mesh.shape["gx"], mesh.shape["gy"])
    return jax.shard_map(
        body,
        mesh=mesh,
        in_specs=(
            P(None, "gx", "gy", None),
            P(None, None, "gx", "gy", None),
            P(None, None, "gx", "gy", None),
            P("gx", "gy", None),
            P("gx", "gy", None),
            P("gx", "gy", None),
            P("gx", "gy", None),
            P("gy", "gx", None, None),
            P("gx", None, "gy", None),
        ),
        out_specs=(P(None, "gx", "gy", None), P("gx", "gy", None)),
        check_vma=False,
    )
```

```python
import functools

import jax
import jax.numpy as jnp
from jax import lax
from jax.experimental import pallas as pl
from jax.experimental.pallas import tpu as pltpu
from jax.sharding import PartitionSpec as P

LANES = 128
COST = 10**10
NT = (((1,), (1,)), ((), ()))


def split3(value):
    top = value.astype(jnp.bfloat16)
    rest = value - top.astype(jnp.float32)
    mid = rest.astype(jnp.bfloat16)
    low = (rest - mid.astype(jnp.float32)).astype(jnp.bfloat16)
    return top, mid, low


def halo_kernel(
    x_index, y_index, field, boundary, inner_out, outer_out, y_out, boundary_out, sems
):
    cells_x, cells_y = field.shape[1], field.shape[2]
    inner = jnp.where(x_index[0] % 2 == 0, cells_x - 1, 0)
    beside = jnp.where(y_index[0] % 2 == 0, cells_y - 1, 0)
    copies = []

    def copy(source, target):
        copies.append(pltpu.make_async_copy(source, target, sems.at[len(copies)]))
        copies[-1].start()

    copy(boundary, boundary_out)
    for slot, comp in enumerate((1, 2)):
        rows = pl.ds(slot * cells_y, cells_y)
        copy(field.at[comp, inner], inner_out.at[rows])
        copy(field.at[comp, cells_x - 1 - inner], outer_out.at[rows])
    for side in range(y_out.shape[0]):
        row = beside if side == 0 else cells_y - 1 - beside
        for slot, comp in enumerate((0, 2)):
            rows = pl.ds(slot * cells_x, cells_x)
            copy(field.at[comp, :, row], y_out.at[side, rows])
    for one in copies:
        one.wait()


def pack_kernel(mine, theirs, out):
    lines = [
        source[:, q * LANES : (q + 1) * LANES]
        for source in (mine, theirs)
        for q in range(mine.shape[1] // LANES)
    ]
    out[...] = jnp.concatenate(lines, axis=0).astype(jnp.bfloat16)


def prepare_kernel(field, boundary, self_term, coupling, owner, placed_out, base_out):
    _, _, _, cells_z = field.shape
    count = boundary.shape[1]
    blocks = count // LANES
    half = blocks // 2
    padded = -(-blocks // 16) * 16

    slot_of = owner[...]
    lane_of = slot_of % LANES
    block_of = slot_of // LANES
    onehot = (
        (lane_of == lax.broadcasted_iota(jnp.int32, (LANES, count), 0))
        .astype(jnp.float32)
        .astype(jnp.bfloat16)
    )
    in_block = block_of == lax.broadcasted_iota(jnp.int32, (padded, count), 0)

    spread = jnp.where(in_block, coupling[...] * boundary[...], 0.0)
    terms = jnp.concatenate(split3(spread), axis=0)
    placed = lax.dot_general(onehot, terms, NT, preferred_element_type=jnp.float32)
    placed_out[...] = (
        placed[:, :padded] + placed[:, padded : 2 * padded] + placed[:, 2 * padded :]
    )

    terms, picks = [], []
    lane = lax.broadcasted_iota(jnp.int32, (cells_z, padded), 1)
    level = lax.broadcasted_iota(jnp.int32, (cells_z, padded), 0)
    flat = field[...].reshape(half, LANES, cells_z)
    for b in range(half):
        chosen = ((level == 0) & (lane == b)) | ((level == cells_z - 1) & (lane == half + b))
        terms += split3(flat[b])
        picks += [chosen.astype(jnp.float32).astype(jnp.bfloat16)] * 3
    table = jnp.dot(
        jnp.concatenate(terms, axis=1),
        jnp.concatenate(picks, axis=0),
        preferred_element_type=jnp.float32,
    )
    table = jnp.concatenate(split3(table.T), axis=0)
    read = jnp.dot(table, onehot, preferred_element_type=jnp.float32)
    read = read[:padded] + read[padded : 2 * padded] + read[2 * padded :]
    trace = jnp.sum(jnp.where(in_block, read, 0.0), axis=0, keepdims=True)
    base_out[...] = self_term[...] * boundary[...] + coupling[...] * trace


def stencil_kernel(
    x_index,
    y_index,
    field,
    diag,
    face,
    x_inner,
    x_outer,
    y_halo,
    placed,
    volume_out,
    result,
    sems,
):
    _, cells_x, cells_y, cells_z = field.shape
    half = 3 * cells_x * cells_y // LANES
    chunk = cells_x // sems.shape[0]
    even_x = x_index[0] % 2 == 0
    even_y = y_index[0] % 2 == 0
    z_at = lax.broadcasted_iota(jnp.int32, (cells_y, cells_z), 1)
    y_at = lax.broadcasted_iota(jnp.int32, (cells_y, cells_z), 0)
    first_z, last_z = z_at == 0, z_at == cells_z - 1
    first_y, last_y = y_at == 0, y_at == cells_y - 1
    stores = []
    for x in range(cells_x):
        own = [field[c, x] for c in range(3)]
        x_plus, x_minus = {}, {}
        for slot, comp in enumerate((1, 2)):
            near = x_inner[slot * cells_y : (slot + 1) * cells_y, :]
            far = x_outer[slot * cells_y : (slot + 1) * cells_y, :]
            if x + 1 < cells_x:
                x_plus[comp] = field[comp, x + 1]
            else:
                x_plus[comp] = jnp.where(even_x, near, far)
            if x > 0:
                x_minus[comp] = field[comp, x - 1]
            else:
                x_minus[comp] = jnp.where(even_x, far, near)
        y_plus, y_minus = {}, {}
        for slot, comp in enumerate((0, 2)):
            at = slot * cells_x + x
            near = y_halo[0, at : at + 1, :]
            if y_halo.shape[0] == 2:
                far = y_halo[1, at : at + 1, :]
            else:
                far = jnp.zeros_like(near)
            above = jnp.where(even_y, near, far)
            below = jnp.where(even_y, far, near)
            y_plus[comp] = jnp.where(last_y, above, pltpu.roll(own[comp], cells_y - 1, 0))
            y_minus[comp] = jnp.where(first_y, below, pltpu.roll(own[comp], 1, 0))
        z_plus, z_minus = {}, {}
        for comp in (0, 1):
            z_plus[comp] = jnp.where(last_z, 0.0, pltpu.roll(own[comp], cells_z - 1, 1))
            z_minus[comp] = jnp.where(first_z, 0.0, pltpu.roll(own[comp], 1, 1))
        total = []
        for comp in range(3):
            total.append(
                diag[comp, 0, x] * own[0] + diag[comp, 1, x] * own[1] + diag[comp, 2, x] * own[2]
            )
        steps = (x_plus, x_minus, y_plus, y_minus, z_plus, z_minus)
        for offset, step in enumerate(steps):
            direction = offset // 2
            for slot, comp in enumerate(c for c in range(3) if c != direction):
                total[comp] = total[comp] - face[offset, slot, x] * step[comp]
        for comp in range(3):
            row = (comp * cells_x + x) * cells_y
            block, at = row // LANES, row % LANES
            bottom = placed[at : at + cells_y, block : block + 1]
            top = placed[at : at + cells_y, half + block : half + block + 1]
            total[comp] = total[comp] + jnp.where(
                first_z, bottom, jnp.where(last_z, top, 0.0)
            )
            result[comp, x] = total[comp]
        if (x + 1) % chunk == 0:
            part = pl.ds(x + 1 - chunk, chunk)
            stores.append(
                pltpu.make_async_copy(
                    result.at[:, part], volume_out.at[:, part], sems.at[len(stores)]
                )
            )
            stores[-1].start()
    for store in stores:
        store.wait()


def integral_kernel(
    steps, x_index, y_index, mine, theirs, right, left, own_out, send_out, stack, partial_value
):
    columns = left.shape[1]
    rank, groups, count = right.shape
    pitch = count // LANES
    held = mine.shape[0]
    stack[0:held, :] = mine[...].astype(jnp.float32)
    stack[held:, :] = theirs[...].astype(jnp.float32)
    pieces = [stack[pl.ds(q, groups, stride=pitch), :] for q in range(pitch)]
    gathered = jnp.concatenate(pieces, axis=1).astype(jnp.bfloat16)
    table = right[...].reshape(rank * groups, count)
    product = lax.dot_general(table, gathered, NT, preferred_element_type=jnp.float32)
    product = product.reshape(rank, groups, groups)
    block = lax.broadcasted_iota(jnp.int32, (rank, groups, groups), 2)
    source = jnp.full((rank, groups, groups), x_index[0], jnp.int32)
    for bit, step in enumerate(steps):
        source = source ^ (((block >> bit) & 1) * step)
    group = lax.broadcasted_iota(jnp.int32, (rank, groups, groups), 1)
    product = jnp.where(source == group, product, 0.0)
    coef = jnp.sum(jnp.sum(product, axis=1, keepdims=True), axis=2, keepdims=True)
    coef = coef.astype(jnp.bfloat16).astype(jnp.float32)
    total = jnp.zeros((columns, count), jnp.float32)
    for r in range(rank):
        total = total + coef[r] * left[r].astype(jnp.float32)
    partial_value[...] = total
    me = y_index[0]
    own_out[...] = partial_value[pl.ds(me, 1), :]
    for step in range(1, columns):
        to = lax.rem(me + step, columns)
        send_out[step - 1] = partial_value[pl.ds(to, 1), :]


def on_device(
    n_x,
    n_y,
    volume_field,
    diag_blocks,
    face_weights,
    boundary_field,
    self_term,
    coupling,
    owner_map,
    left_basis,
    right_basis,
):
    f32 = jnp.float32
    _, cells_x, cells_y, _ = volume_field.shape
    count = boundary_field.shape[2]
    rank = left_basis.shape[0]
    rows = count // LANES
    row = (1, count)
    head = -(-rows // 16) * 16
    x_index = lax.axis_index("gx").reshape(1)
    y_index = lax.axis_index("gy").reshape(1)
    boundary = boundary_field.reshape(1, count)
    vmem = pl.BlockSpec(memory_space=pltpu.VMEM)
    smem = pl.BlockSpec(memory_space=pltpu.SMEM)
    hbm = pl.BlockSpec(memory_space=pltpu.HBM)
    y_sides = 1 if n_y == 2 else 2

    def call(body, outs, args, scratch=(), far=0, indices=True, far_outs=0, cost=0):
        lead = (x_index, y_index) if indices else ()
        args = [
            pltpu.with_memory_space_constraint(arg, pltpu.HBM if i < far else pltpu.VMEM)
            for i, arg in enumerate(args)
        ]
        return pl.pallas_call(
            body,
            out_shape=outs,
            in_specs=[smem] * len(lead) + [hbm] * far + [vmem] * (len(args) - far),
            out_specs=[hbm] * far_outs + [vmem] * (len(outs) - far_outs),
            scratch_shapes=scratch,
            compiler_params=pltpu.CompilerParams(vmem_limit_bytes=16 * 2**20),
            cost_estimate=pl.CostEstimate(flops=cost, transcendentals=0, bytes_accessed=0),
        )(*lead, *args)

    def inner_pairs(size):
        return [(i, i ^ 1) for i in range(size)]

    def outer_pairs(size):
        up = [(i, i + 1) for i in range(1, size - 1, 2)]
        return up + [(j, i) for i, j in up]

    core_got = lax.ppermute(boundary, "gx", inner_pairs(n_x))
    inner_pay, outer_pay, y_pay, near_boundary = call(
        halo_kernel,
        [
            pltpu.VMEM((2 * cells_y, LANES), f32),
            pltpu.VMEM((2 * cells_y, LANES), f32),
            pltpu.VMEM((y_sides, 2 * cells_x, LANES), f32),
            pltpu.VMEM(row, f32),
        ],
        [volume_field, boundary],
        [pltpu.SemaphoreType.DMA((5 + 2 * y_sides,))],
        far=2,
        cost=COST,
    )
    x_inner = lax.ppermute(inner_pay, "gx", inner_pairs(n_x))
    x_outer = lax.ppermute(outer_pay, "gx", outer_pairs(n_x))
    y_halo = lax.ppermute(y_pay[0], "gy", inner_pairs(n_y))[None]
    if y_sides == 2:
        y_far = lax.ppermute(y_pay[1], "gy", outer_pairs(n_y))[None]
        y_halo = jnp.concatenate([y_halo, y_far], axis=0)

    (mine,) = call(
        pack_kernel,
        [pltpu.VMEM((2 * rows, LANES), jnp.bfloat16)],
        [near_boundary, core_got],
        indices=False,
    )
    steps = [1]
    step = 2
    while step < n_x:
        steps.append(step)
        pairs = [(i, i ^ step) for i in range(n_x)]
        theirs = lax.ppermute(mine, "gx", pairs)
        if 2 * step < n_x:
            mine = jnp.concatenate([mine, theirs], axis=0)
        step *= 2

    placed, base = call(
        prepare_kernel,
        [pltpu.VMEM((LANES, head), f32), pltpu.VMEM(row, f32)],
        [
            volume_field,
            near_boundary,
            self_term.reshape(row),
            coupling.reshape(row),
            owner_map.reshape(row),
        ],
        indices=False,
        cost=COST,
    )

    own, shares = call(
        functools.partial(integral_kernel, tuple(steps)),
        [pltpu.VMEM(row, f32), pltpu.VMEM((n_y - 1, 1, count), f32)],
        [
            mine,
            theirs,
            right_basis.reshape(rank, n_x, count),
            left_basis.reshape(rank, n_y, count),
        ],
        [
            pltpu.VMEM((n_x * rows, LANES), f32),
            pltpu.VMEM((n_y, count), f32),
        ],
        cost=COST,
    )

    (volume_out,) = call(
        stencil_kernel,
        [jax.ShapeDtypeStruct(volume_field.shape, f32)],
        [volume_field, diag_blocks, face_weights, x_inner, x_outer, y_halo, placed],
        [pltpu.VMEM(volume_field.shape, f32), pltpu.SemaphoreType.DMA((4,))],
        far_outs=1,
        cost=COST,
    )
    total = base + own
    for shift in range(1, n_y):
        pairs = [(i, (i + shift) % n_y) for i in range(n_y)]
        total = total + lax.ppermute(shares[shift - 1], "gy", pairs)
    return volume_out, total.reshape(boundary_field.shape)


def solution(mesh):
    body = functools.partial(on_device, mesh.shape["gx"], mesh.shape["gy"])
    return jax.shard_map(
        body,
        mesh=mesh,
        in_specs=(
            P(None, "gx", "gy", None),
            P(None, None, "gx", "gy", None),
            P(None, None, "gx", "gy", None),
            P("gx", "gy", None),
            P("gx", "gy", None),
            P("gx", "gy", None),
            P("gx", "gy", None),
            P("gy", "gx", None, None),
            P("gx", None, "gy", None),
        ),
        out_specs=(P(None, "gx", "gy", None), P("gx", "gy", None)),
        check_vma=False,
    )
```

```python
import functools

import jax
import jax.numpy as jnp
from jax import lax
from jax.experimental import pallas as pl
from jax.experimental.pallas import tpu as pltpu
from jax.sharding import PartitionSpec as P

LANES = 128
COST = 10**10
NT = (((1,), (1,)), ((), ()))


def split3(value):
    top = value.astype(jnp.bfloat16)
    rest = value - top.astype(jnp.float32)
    mid = rest.astype(jnp.bfloat16)
    low = (rest - mid.astype(jnp.float32)).astype(jnp.bfloat16)
    return top, mid, low


def halo_kernel(
    x_index, y_index, field, boundary, inner_out, outer_out, y_out, boundary_out, inner, sems
):
    cells_x, cells_y = field.shape[1], field.shape[2]
    at_inner = jnp.where(x_index[0] % 2 == 0, cells_x - 1, 0)
    beside = jnp.where(y_index[0] % 2 == 0, cells_y - 1, 0)
    copies = []

    def copy(source, target):
        copies.append(pltpu.make_async_copy(source, target, sems.at[len(copies)]))
        copies[-1].start()

    copy(boundary, boundary_out)
    for slot, comp in enumerate((1, 2)):
        rows = pl.ds(slot * cells_y, cells_y)
        copy(field.at[comp, at_inner], inner.at[rows])
        copy(field.at[comp, cells_x - 1 - at_inner], outer_out.at[rows])
    for side in range(y_out.shape[0]):
        row = beside if side == 0 else cells_y - 1 - beside
        for slot, comp in enumerate((0, 2)):
            rows = pl.ds(slot * cells_x, cells_x)
            copy(field.at[comp, :, row], y_out.at[side, rows])
    for one in copies:
        one.wait()
    inner_out[...] = jnp.concatenate(split3(inner[...]), axis=0)


def pack_kernel(mine, theirs, out):
    lines = [
        source[:, q * LANES : (q + 1) * LANES]
        for source in (mine, theirs)
        for q in range(mine.shape[1] // LANES)
    ]
    out[...] = jnp.concatenate(lines, axis=0).astype(jnp.bfloat16)


def prepare_kernel(field, boundary, self_term, coupling, owner, placed_out, base_out):
    _, _, _, cells_z = field.shape
    count = boundary.shape[1]
    blocks = count // LANES
    half = blocks // 2
    padded = -(-blocks // 16) * 16

    slot_of = owner[...]
    lane_of = slot_of % LANES
    block_of = slot_of // LANES
    onehot = (
        (lane_of == lax.broadcasted_iota(jnp.int32, (LANES, count), 0))
        .astype(jnp.float32)
        .astype(jnp.bfloat16)
    )
    in_block = block_of == lax.broadcasted_iota(jnp.int32, (padded, count), 0)

    spread = jnp.where(in_block, coupling[...] * boundary[...], 0.0)
    terms = jnp.concatenate(split3(spread), axis=0)
    placed = lax.dot_general(onehot, terms, NT, preferred_element_type=jnp.float32)
    placed_out[...] = (
        placed[:, :padded] + placed[:, padded : 2 * padded] + placed[:, 2 * padded :]
    )

    terms, picks = [], []
    lane = lax.broadcasted_iota(jnp.int32, (cells_z, padded), 1)
    level = lax.broadcasted_iota(jnp.int32, (cells_z, padded), 0)
    flat = field[...].reshape(half, LANES, cells_z)
    for b in range(half):
        chosen = ((level == 0) & (lane == b)) | ((level == cells_z - 1) & (lane == half + b))
        terms += split3(flat[b])
        picks += [chosen.astype(jnp.float32).astype(jnp.bfloat16)] * 3
    table = jnp.dot(
        jnp.concatenate(terms, axis=1),
        jnp.concatenate(picks, axis=0),
        preferred_element_type=jnp.float32,
    )
    table = jnp.concatenate(split3(table.T), axis=0)
    read = jnp.dot(table, onehot, preferred_element_type=jnp.float32)
    read = read[:padded] + read[padded : 2 * padded] + read[2 * padded :]
    trace = jnp.sum(jnp.where(in_block, read, 0.0), axis=0, keepdims=True)
    base_out[...] = self_term[...] * boundary[...] + coupling[...] * trace


def stencil_kernel(
    x_index,
    y_index,
    field,
    diag,
    face,
    from_core,
    x_outer,
    y_halo,
    placed,
    volume_out,
    result,
    sems,
):
    _, cells_x, cells_y, cells_z = field.shape
    half = 3 * cells_x * cells_y // LANES
    chunk = cells_x // sems.shape[0]
    even_x = x_index[0] % 2 == 0
    even_y = y_index[0] % 2 == 0
    z_at = lax.broadcasted_iota(jnp.int32, (cells_y, cells_z), 1)
    y_at = lax.broadcasted_iota(jnp.int32, (cells_y, cells_z), 0)
    first_z, last_z = z_at == 0, z_at == cells_z - 1
    first_y, last_y = y_at == 0, y_at == cells_y - 1
    faces = 2 * cells_y
    first_term = from_core.shape[0] - 3 * faces
    terms = [
        from_core[first_term + term * faces : first_term + (term + 1) * faces, :]
        for term in range(3)
    ]
    terms = [term.astype(jnp.float32) for term in terms]
    near_rows = (terms[0] + terms[1]) + terms[2]
    stores = []
    for x in range(cells_x):
        own = [field[c, x] for c in range(3)]
        x_plus, x_minus = {}, {}
        for slot, comp in enumerate((1, 2)):
            near = near_rows[slot * cells_y : (slot + 1) * cells_y, :]
            far = x_outer[slot * cells_y : (slot + 1) * cells_y, :]
            if x + 1 < cells_x:
                x_plus[comp] = field[comp, x + 1]
            else:
                x_plus[comp] = jnp.where(even_x, near, far)
            if x > 0:
                x_minus[comp] = field[comp, x - 1]
            else:
                x_minus[comp] = jnp.where(even_x, far, near)
        y_plus, y_minus = {}, {}
        for slot, comp in enumerate((0, 2)):
            at = slot * cells_x + x
            near = y_halo[0, at : at + 1, :]
            if y_halo.shape[0] == 2:
                far = y_halo[1, at : at + 1, :]
            else:
                far = jnp.zeros_like(near)
            above = jnp.where(even_y, near, far)
            below = jnp.where(even_y, far, near)
            y_plus[comp] = jnp.where(last_y, above, pltpu.roll(own[comp], cells_y - 1, 0))
            y_minus[comp] = jnp.where(first_y, below, pltpu.roll(own[comp], 1, 0))
        z_plus, z_minus = {}, {}
        for comp in (0, 1):
            z_plus[comp] = jnp.where(last_z, 0.0, pltpu.roll(own[comp], cells_z - 1, 1))
            z_minus[comp] = jnp.where(first_z, 0.0, pltpu.roll(own[comp], 1, 1))
        total = []
        for comp in range(3):
            total.append(
                diag[comp, 0, x] * own[0] + diag[comp, 1, x] * own[1] + diag[comp, 2, x] * own[2]
            )
        steps = (x_plus, x_minus, y_plus, y_minus, z_plus, z_minus)
        for offset, step in enumerate(steps):
            direction = offset // 2
            for slot, comp in enumerate(c for c in range(3) if c != direction):
                total[comp] = total[comp] - face[offset, slot, x] * step[comp]
        for comp in range(3):
            row = (comp * cells_x + x) * cells_y
            block, at = row // LANES, row % LANES
            bottom = placed[at : at + cells_y, block : block + 1]
            top = placed[at : at + cells_y, half + block : half + block + 1]
            total[comp] = total[comp] + jnp.where(
                first_z, bottom, jnp.where(last_z, top, 0.0)
            )
            result[comp, x] = total[comp]
        if (x + 1) % chunk == 0:
            part = pl.ds(x + 1 - chunk, chunk)
            stores.append(
                pltpu.make_async_copy(
                    result.at[:, part], volume_out.at[:, part], sems.at[len(stores)]
                )
            )
            stores[-1].start()
    for store in stores:
        store.wait()


def integral_kernel(
    steps,
    x_index,
    y_index,
    held,
    got,
    cross,
    from_core,
    right,
    left,
    own_out,
    send_out,
    stack,
    partial_value,
):
    columns = left.shape[1]
    rank, groups, count = right.shape
    pitch = count // LANES
    size = held.shape[0]
    for i, piece in enumerate((held, got, cross, from_core)):
        stack[i * size : (i + 1) * size, :] = piece[0:size, :].astype(jnp.float32)
    pieces = [stack[pl.ds(q, groups, stride=pitch), :] for q in range(pitch)]
    gathered = jnp.concatenate(pieces, axis=1).astype(jnp.bfloat16)
    table = right[...].reshape(rank * groups, count)
    product = lax.dot_general(table, gathered, NT, preferred_element_type=jnp.float32)
    product = product.reshape(rank, groups, groups)
    block = lax.broadcasted_iota(jnp.int32, (rank, groups, groups), 2)
    source = jnp.full((rank, groups, groups), x_index[0], jnp.int32)
    for bit, step in enumerate(steps):
        source = source ^ (((block >> bit) & 1) * step)
    piece = block >> len(steps)
    mask = jnp.where(x_index[0] % 2 == 0, 2, 4)
    source = source ^ jnp.where(piece == 1, mask, 0)
    source = source ^ jnp.where(piece == 2, 6, 0)
    source = source ^ jnp.where(piece == 3, (6 - mask) ^ 1, 0)
    group = lax.broadcasted_iota(jnp.int32, (rank, groups, groups), 1)
    product = jnp.where(source == group, product, 0.0)
    coef = jnp.sum(jnp.sum(product, axis=1, keepdims=True), axis=2, keepdims=True)
    coef = coef.astype(jnp.bfloat16).astype(jnp.float32)
    total = jnp.zeros((columns, count), jnp.float32)
    for r in range(rank):
        total = total + coef[r] * left[r].astype(jnp.float32)
    partial_value[...] = total
    me = y_index[0]
    own_out[...] = partial_value[pl.ds(me, 1), :]
    for step in range(1, columns):
        to = lax.rem(me + step, columns)
        send_out[step - 1] = partial_value[pl.ds(to, 1), :]


def on_device(
    n_x,
    n_y,
    volume_field,
    diag_blocks,
    face_weights,
    boundary_field,
    self_term,
    coupling,
    owner_map,
    left_basis,
    right_basis,
):
    f32 = jnp.float32
    _, cells_x, cells_y, _ = volume_field.shape
    count = boundary_field.shape[2]
    rank = left_basis.shape[0]
    rows = count // LANES
    row = (1, count)
    head = -(-rows // 16) * 16
    x_index = lax.axis_index("gx").reshape(1)
    y_index = lax.axis_index("gy").reshape(1)
    boundary = boundary_field.reshape(1, count)
    vmem = pl.BlockSpec(memory_space=pltpu.VMEM)
    smem = pl.BlockSpec(memory_space=pltpu.SMEM)
    hbm = pl.BlockSpec(memory_space=pltpu.HBM)
    y_sides = 1 if n_y == 2 else 2

    def call(body, outs, args, scratch=(), far=0, indices=True, far_outs=0, cost=0):
        lead = (x_index, y_index) if indices else ()
        args = [
            pltpu.with_memory_space_constraint(arg, pltpu.HBM if i < far else pltpu.VMEM)
            for i, arg in enumerate(args)
        ]
        return pl.pallas_call(
            body,
            out_shape=outs,
            in_specs=[smem] * len(lead) + [hbm] * far + [vmem] * (len(args) - far),
            out_specs=[hbm] * far_outs + [vmem] * (len(outs) - far_outs),
            scratch_shapes=scratch,
            compiler_params=pltpu.CompilerParams(vmem_limit_bytes=16 * 2**20),
            cost_estimate=pl.CostEstimate(flops=cost, transcendentals=0, bytes_accessed=0),
        )(*lead, *args)

    def inner_pairs(size):
        return [(i, i ^ 1) for i in range(size)]

    def outer_pairs(size):
        up = [(i, i + 1) for i in range(1, size - 1, 2)]
        return up + [(j, i) for i, j in up]

    def xor_pairs(step, odd_step=None):
        return [(i, i ^ (odd_step if odd_step and i % 2 else step)) for i in range(n_x)]

    got = lax.ppermute(boundary, "gx", xor_pairs(1))
    inner_pay, outer_pay, y_pay, near_boundary = call(
        halo_kernel,
        [
            pltpu.VMEM((3 * 2 * cells_y, LANES), jnp.bfloat16),
            pltpu.VMEM((2 * cells_y, LANES), f32),
            pltpu.VMEM((y_sides, 2 * cells_x, LANES), f32),
            pltpu.VMEM(row, f32),
        ],
        [volume_field, boundary],
        [
            pltpu.VMEM((2 * cells_y, LANES), f32),
            pltpu.SemaphoreType.DMA((5 + 2 * y_sides,)),
        ],
        far=2,
        cost=COST,
    )
    x_outer = lax.ppermute(outer_pay, "gx", outer_pairs(n_x))
    y_halo = lax.ppermute(y_pay[0], "gy", inner_pairs(n_y))[None]
    if y_sides == 2:
        y_far = lax.ppermute(y_pay[1], "gy", outer_pairs(n_y))[None]
        y_halo = jnp.concatenate([y_halo, y_far], axis=0)
    (held,) = call(
        pack_kernel,
        [pltpu.VMEM((2 * rows, LANES), jnp.bfloat16)],
        [near_boundary, got],
        indices=False,
    )
    steps = [1]
    step = n_x // 2
    while step > 4:
        steps.append(step)
        got = lax.ppermute(held, "gx", xor_pairs(step))
        held = jnp.concatenate([held, got], axis=0)
        step //= 2
    cross = lax.ppermute(held, "gx", xor_pairs(6))
    got = lax.ppermute(held, "gx", xor_pairs(2, 4))
    from_core = lax.ppermute(
        jnp.concatenate([got, inner_pay], axis=0), "gx", xor_pairs(1)
    )

    placed, base = call(
        prepare_kernel,
        [pltpu.VMEM((LANES, head), f32), pltpu.VMEM(row, f32)],
        [
            volume_field,
            near_boundary,
            self_term.reshape(row),
            coupling.reshape(row),
            owner_map.reshape(row),
        ],
        indices=False,
        cost=COST,
    )

    own, shares = call(
        functools.partial(integral_kernel, tuple(steps)),
        [pltpu.VMEM(row, f32), pltpu.VMEM((n_y - 1, 1, count), f32)],
        [
            held,
            got,
            cross,
            from_core,
            right_basis.reshape(rank, n_x, count),
            left_basis.reshape(rank, n_y, count),
        ],
        [
            pltpu.VMEM((n_x * rows, LANES), f32),
            pltpu.VMEM((n_y, count), f32),
        ],
        cost=COST,
    )

    (volume_out,) = call(
        stencil_kernel,
        [jax.ShapeDtypeStruct(volume_field.shape, f32)],
        [volume_field, diag_blocks, face_weights, from_core, x_outer, y_halo, placed],
        [pltpu.VMEM(volume_field.shape, f32), pltpu.SemaphoreType.DMA((4,))],
        far_outs=1,
        cost=COST,
    )
    total = base + own
    for shift in range(1, n_y):
        pairs = [(i, (i + shift) % n_y) for i in range(n_y)]
        total = total + lax.ppermute(shares[shift - 1], "gy", pairs)
    return volume_out, total.reshape(boundary_field.shape)


def solution(mesh):
    body = functools.partial(on_device, mesh.shape["gx"], mesh.shape["gy"])
    return jax.shard_map(
        body,
        mesh=mesh,
        in_specs=(
            P(None, "gx", "gy", None),
            P(None, None, "gx", "gy", None),
            P(None, None, "gx", "gy", None),
            P("gx", "gy", None),
            P("gx", "gy", None),
            P("gx", "gy", None),
            P("gx", "gy", None),
            P("gy", "gx", None, None),
            P("gx", None, "gy", None),
        ),
        out_specs=(P(None, "gx", "gy", None), P("gx", "gy", None)),
        check_vma=False,
    )
```

```python
import functools

import jax
import jax.numpy as jnp
from jax import lax
from jax.experimental import pallas as pl
from jax.experimental.pallas import tpu as pltpu
from jax.sharding import PartitionSpec as P

LANES = 128
COST = 10**10
NT = (((1,), (1,)), ((), ()))


def split3(value):
    top = value.astype(jnp.bfloat16)
    rest = value - top.astype(jnp.float32)
    mid = rest.astype(jnp.bfloat16)
    low = (rest - mid.astype(jnp.float32)).astype(jnp.bfloat16)
    return top, mid, low


def halo_kernel(
    x_index, y_index, field, boundary, inner_out, outer_out, y_out, boundary_out, inner, sems
):
    cells_x, cells_y = field.shape[1], field.shape[2]
    at_inner = jnp.where(x_index[0] % 2 == 0, cells_x - 1, 0)
    beside = jnp.where(y_index[0] % 2 == 0, cells_y - 1, 0)
    copies = []

    def copy(source, target):
        copies.append(pltpu.make_async_copy(source, target, sems.at[len(copies)]))
        copies[-1].start()

    copy(boundary, boundary_out)
    for slot, comp in enumerate((1, 2)):
        rows = pl.ds(slot * cells_y, cells_y)
        copy(field.at[comp, at_inner], inner.at[rows])
        copy(field.at[comp, cells_x - 1 - at_inner], outer_out.at[rows])
    for side in range(y_out.shape[0]):
        row = beside if side == 0 else cells_y - 1 - beside
        for slot, comp in enumerate((0, 2)):
            rows = pl.ds(slot * cells_x, cells_x)
            copy(field.at[comp, :, row], y_out.at[side, rows])
    for one in copies:
        one.wait()
    inner_out[...] = jnp.concatenate(split3(inner[...]), axis=0)


def pack_kernel(mine, theirs, out):
    lines = [
        source[:, q * LANES : (q + 1) * LANES]
        for source in (mine, theirs)
        for q in range(mine.shape[1] // LANES)
    ]
    out[...] = jnp.concatenate(lines, axis=0).astype(jnp.bfloat16)


def prepare_kernel(field, boundary, self_term, coupling, owner, placed_out, base_out):
    _, _, _, cells_z = field.shape
    count = boundary.shape[1]
    blocks = count // LANES
    half = blocks // 2
    padded = -(-blocks // 16) * 16

    slot_of = owner[...]
    lane_of = slot_of % LANES
    block_of = slot_of // LANES
    onehot = (
        (lane_of == lax.broadcasted_iota(jnp.int32, (LANES, count), 0))
        .astype(jnp.float32)
        .astype(jnp.bfloat16)
    )
    in_block = block_of == lax.broadcasted_iota(jnp.int32, (padded, count), 0)

    spread = jnp.where(in_block, coupling[...] * boundary[...], 0.0)
    terms = jnp.concatenate(split3(spread), axis=0)
    placed = lax.dot_general(onehot, terms, NT, preferred_element_type=jnp.float32)
    placed_out[...] = (
        placed[:, :padded] + placed[:, padded : 2 * padded] + placed[:, 2 * padded :]
    )

    terms, picks = [], []
    lane = lax.broadcasted_iota(jnp.int32, (cells_z, padded), 1)
    level = lax.broadcasted_iota(jnp.int32, (cells_z, padded), 0)
    flat = field[...].reshape(half, LANES, cells_z)
    for b in range(half):
        chosen = ((level == 0) & (lane == b)) | ((level == cells_z - 1) & (lane == half + b))
        terms += split3(flat[b])
        picks += [chosen.astype(jnp.float32).astype(jnp.bfloat16)] * 3
    table = jnp.dot(
        jnp.concatenate(terms, axis=1),
        jnp.concatenate(picks, axis=0),
        preferred_element_type=jnp.float32,
    )
    table = jnp.concatenate(split3(table.T), axis=0)
    read = jnp.dot(table, onehot, preferred_element_type=jnp.float32)
    read = read[:padded] + read[padded : 2 * padded] + read[2 * padded :]
    trace = jnp.sum(jnp.where(in_block, read, 0.0), axis=0, keepdims=True)
    base_out[...] = self_term[...] * boundary[...] + coupling[...] * trace


def stencil_kernel(
    x_index,
    y_index,
    field,
    diag,
    face,
    from_core,
    x_outer,
    y_halo,
    placed,
    volume_out,
    result,
    sems,
):
    _, cells_x, cells_y, cells_z = field.shape
    half = 3 * cells_x * cells_y // LANES
    chunk = cells_x // sems.shape[0]
    even_x = x_index[0] % 2 == 0
    even_y = y_index[0] % 2 == 0
    z_at = lax.broadcasted_iota(jnp.int32, (cells_y, cells_z), 1)
    y_at = lax.broadcasted_iota(jnp.int32, (cells_y, cells_z), 0)
    first_z, last_z = z_at == 0, z_at == cells_z - 1
    first_y, last_y = y_at == 0, y_at == cells_y - 1
    faces = 2 * cells_y
    first_term = from_core.shape[0] - 3 * faces
    terms = [
        from_core[first_term + term * faces : first_term + (term + 1) * faces, :]
        for term in range(3)
    ]
    terms = [term.astype(jnp.float32) for term in terms]
    near_rows = (terms[0] + terms[1]) + terms[2]
    stores = []
    for x in range(cells_x):
        own = [field[c, x] for c in range(3)]
        x_plus, x_minus = {}, {}
        for slot, comp in enumerate((1, 2)):
            near = near_rows[slot * cells_y : (slot + 1) * cells_y, :]
            far = x_outer[slot * cells_y : (slot + 1) * cells_y, :]
            if x + 1 < cells_x:
                x_plus[comp] = field[comp, x + 1]
            else:
                x_plus[comp] = jnp.where(even_x, near, far)
            if x > 0:
                x_minus[comp] = field[comp, x - 1]
            else:
                x_minus[comp] = jnp.where(even_x, far, near)
        y_plus, y_minus = {}, {}
        for slot, comp in enumerate((0, 2)):
            at = slot * cells_x + x
            near = y_halo[0, at : at + 1, :]
            if y_halo.shape[0] == 2:
                far = y_halo[1, at : at + 1, :]
            else:
                far = jnp.zeros_like(near)
            above = jnp.where(even_y, near, far)
            below = jnp.where(even_y, far, near)
            y_plus[comp] = jnp.where(last_y, above, pltpu.roll(own[comp], cells_y - 1, 0))
            y_minus[comp] = jnp.where(first_y, below, pltpu.roll(own[comp], 1, 0))
        z_plus, z_minus = {}, {}
        for comp in (0, 1):
            z_plus[comp] = jnp.where(last_z, 0.0, pltpu.roll(own[comp], cells_z - 1, 1))
            z_minus[comp] = jnp.where(first_z, 0.0, pltpu.roll(own[comp], 1, 1))
        total = []
        for comp in range(3):
            total.append(
                diag[comp, 0, x] * own[0] + diag[comp, 1, x] * own[1] + diag[comp, 2, x] * own[2]
            )
        steps = (x_plus, x_minus, y_plus, y_minus, z_plus, z_minus)
        for offset, step in enumerate(steps):
            direction = offset // 2
            for slot, comp in enumerate(c for c in range(3) if c != direction):
                total[comp] = total[comp] - face[offset, slot, x] * step[comp]
        for comp in range(3):
            row = (comp * cells_x + x) * cells_y
            block, at = row // LANES, row % LANES
            bottom = placed[at : at + cells_y, block : block + 1]
            top = placed[at : at + cells_y, half + block : half + block + 1]
            total[comp] = total[comp] + jnp.where(
                first_z, bottom, jnp.where(last_z, top, 0.0)
            )
            result[comp, x] = total[comp]
        if (x + 1) % chunk == 0:
            part = pl.ds(x + 1 - chunk, chunk)
            stores.append(
                pltpu.make_async_copy(
                    result.at[:, part], volume_out.at[:, part], sems.at[len(stores)]
                )
            )
            stores[-1].start()
    for store in stores:
        store.wait()


def integral_kernel(masks, x_index, y_index, held, *rest):
    pieces, rest = (held,) + rest[: len(masks)], rest[len(masks) :]
    from_core, right, left, own_out, send_out, stack, partial_value = rest
    columns = left.shape[1]
    rank, groups, count = right.shape
    pitch = count // LANES
    size = held.shape[0]
    at = 0
    for piece in pieces:
        stack[at : at + size, :] = piece[...].astype(jnp.float32)
        at += size
    stack[at:, :] = from_core[0 : groups * pitch - at, :].astype(jnp.float32)
    lines = [stack[pl.ds(q, groups, stride=pitch), :] for q in range(pitch)]
    gathered = jnp.concatenate(lines, axis=1).astype(jnp.bfloat16)
    table = right[...].reshape(rank * groups, count)
    product = lax.dot_general(table, gathered, NT, preferred_element_type=jnp.float32)
    product = product.reshape(rank, groups, groups)
    block = lax.broadcasted_iota(jnp.int32, (rank, groups, groups), 2)
    piece = block // 2
    odd = x_index[0] % 2 == 1
    source = (block % 2) ^ x_index[0]
    for i, (even_mask, odd_mask) in enumerate(masks):
        source = source ^ jnp.where(piece == i + 1, jnp.where(odd, odd_mask, even_mask), 0)
    for i, (even_mask, odd_mask) in enumerate(masks[:-1]):
        mask = jnp.where(odd, even_mask, odd_mask) ^ 1
        source = source ^ jnp.where(piece == len(masks) + 1 + i, mask, 0)
    group = lax.broadcasted_iota(jnp.int32, (rank, groups, groups), 1)
    product = jnp.where(source == group, product, 0.0)
    coef = jnp.sum(jnp.sum(product, axis=1, keepdims=True), axis=2, keepdims=True)
    coef = coef.astype(jnp.bfloat16).astype(jnp.float32)
    total = jnp.zeros((columns, count), jnp.float32)
    for r in range(rank):
        total = total + coef[r] * left[r].astype(jnp.float32)
    partial_value[...] = total
    me = y_index[0]
    own_out[...] = partial_value[pl.ds(me, 1), :]
    for step in range(1, columns):
        to = lax.rem(me + step, columns)
        send_out[step - 1] = partial_value[pl.ds(to, 1), :]


def on_device(
    n_x,
    n_y,
    volume_field,
    diag_blocks,
    face_weights,
    boundary_field,
    self_term,
    coupling,
    owner_map,
    left_basis,
    right_basis,
):
    f32 = jnp.float32
    _, cells_x, cells_y, _ = volume_field.shape
    count = boundary_field.shape[2]
    rank = left_basis.shape[0]
    rows = count // LANES
    row = (1, count)
    head = -(-rows // 16) * 16
    x_index = lax.axis_index("gx").reshape(1)
    y_index = lax.axis_index("gy").reshape(1)
    boundary = boundary_field.reshape(1, count)
    vmem = pl.BlockSpec(memory_space=pltpu.VMEM)
    smem = pl.BlockSpec(memory_space=pltpu.SMEM)
    hbm = pl.BlockSpec(memory_space=pltpu.HBM)
    y_sides = 1 if n_y == 2 else 2

    def call(body, outs, args, scratch=(), far=0, indices=True, far_outs=0, cost=0):
        lead = (x_index, y_index) if indices else ()
        args = [
            pltpu.with_memory_space_constraint(arg, pltpu.HBM if i < far else pltpu.VMEM)
            for i, arg in enumerate(args)
        ]
        return pl.pallas_call(
            body,
            out_shape=outs,
            in_specs=[smem] * len(lead) + [hbm] * far + [vmem] * (len(args) - far),
            out_specs=[hbm] * far_outs + [vmem] * (len(outs) - far_outs),
            scratch_shapes=scratch,
            compiler_params=pltpu.CompilerParams(vmem_limit_bytes=16 * 2**20),
            cost_estimate=pl.CostEstimate(flops=cost, transcendentals=0, bytes_accessed=0),
        )(*lead, *args)

    def inner_pairs(size):
        return [(i, i ^ 1) for i in range(size)]

    def outer_pairs(size):
        up = [(i, i + 1) for i in range(1, size - 1, 2)]
        return up + [(j, i) for i, j in up]

    def xor_pairs(step, odd_step=None):
        return [(i, i ^ (odd_step if odd_step and i % 2 else step)) for i in range(n_x)]

    got = lax.ppermute(boundary, "gx", xor_pairs(1))
    inner_pay, outer_pay, y_pay, near_boundary = call(
        halo_kernel,
        [
            pltpu.VMEM((3 * 2 * cells_y, LANES), jnp.bfloat16),
            pltpu.VMEM((2 * cells_y, LANES), f32),
            pltpu.VMEM((y_sides, 2 * cells_x, LANES), f32),
            pltpu.VMEM(row, f32),
        ],
        [volume_field, boundary],
        [
            pltpu.VMEM((2 * cells_y, LANES), f32),
            pltpu.SemaphoreType.DMA((5 + 2 * y_sides,)),
        ],
        far=2,
        cost=COST,
    )
    x_outer = lax.ppermute(outer_pay, "gx", outer_pairs(n_x))
    y_halo = lax.ppermute(y_pay[0], "gy", inner_pairs(n_y))[None]
    if y_sides == 2:
        y_far = lax.ppermute(y_pay[1], "gy", outer_pairs(n_y))[None]
        y_halo = jnp.concatenate([y_halo, y_far], axis=0)
    (held,) = call(
        pack_kernel,
        [pltpu.VMEM((2 * rows, LANES), jnp.bfloat16)],
        [near_boundary, got],
        indices=False,
    )
    evens = list(range(n_x - 4, 0, -4))
    evens[0], evens[1] = evens[1], evens[0]
    masks = [(step, step + 2) for step in evens] + [(2, 2)]
    gots = [lax.ppermute(held, "gx", xor_pairs(even, odd)) for even, odd in masks]
    from_core = lax.ppermute(jnp.concatenate(gots[:-1] + [inner_pay], axis=0), "gx", xor_pairs(1))

    placed, base = call(
        prepare_kernel,
        [pltpu.VMEM((LANES, head), f32), pltpu.VMEM(row, f32)],
        [
            volume_field,
            near_boundary,
            self_term.reshape(row),
            coupling.reshape(row),
            owner_map.reshape(row),
        ],
        indices=False,
        cost=COST,
    )

    own, shares = call(
        functools.partial(integral_kernel, tuple(masks)),
        [pltpu.VMEM(row, f32), pltpu.VMEM((n_y - 1, 1, count), f32)],
        [
            held,
            *gots,
            from_core,
            right_basis.reshape(rank, n_x, count),
            left_basis.reshape(rank, n_y, count),
        ],
        [
            pltpu.VMEM((n_x * rows, LANES), f32),
            pltpu.VMEM((n_y, count), f32),
        ],
        cost=COST,
    )

    (volume_out,) = call(
        stencil_kernel,
        [jax.ShapeDtypeStruct(volume_field.shape, f32)],
        [volume_field, diag_blocks, face_weights, from_core, x_outer, y_halo, placed],
        [pltpu.VMEM(volume_field.shape, f32), pltpu.SemaphoreType.DMA((4,))],
        far_outs=1,
        cost=COST,
    )
    total = base + own
    for shift in range(1, n_y):
        pairs = [(i, (i + shift) % n_y) for i in range(n_y)]
        total = total + lax.ppermute(shares[shift - 1], "gy", pairs)
    return volume_out, total.reshape(boundary_field.shape)


def solution(mesh):
    body = functools.partial(on_device, mesh.shape["gx"], mesh.shape["gy"])
    return jax.shard_map(
        body,
        mesh=mesh,
        in_specs=(
            P(None, "gx", "gy", None),
            P(None, None, "gx", "gy", None),
            P(None, None, "gx", "gy", None),
            P("gx", "gy", None),
            P("gx", "gy", None),
            P("gx", "gy", None),
            P("gx", "gy", None),
            P("gy", "gx", None, None),
            P("gx", None, "gy", None),
        ),
        out_specs=(P(None, "gx", "gy", None), P("gx", "gy", None)),
        check_vma=False,
    )
```
